32 devices in a mesh: scen: 8 (over y, x, core), veh: 4 (over z).
Axes of the slice: x: 2, y: 2, z: 4, core: 2. Of those that a mesh axis runs over, the one named last changes fastest.
Arguments:
- start_plan: bfloat16 [128, 3584, 128], P('scen', 'veh'), may hold values from -6 to 6
- linear_cost: bfloat16 [128, 3584, 128], P('scen', 'veh'), may hold values from -12 to 12
- price: bfloat16 [128, 3584, 128], P('scen', 'veh'), may hold values from -6 to 6
- anchor: bfloat16 [8, 3584, 128], P(None, 'veh'), may hold values from -6 to 6
- hessian: bfloat16 [128, 128, 128], P('scen'), as said below
- usage_coef: bfloat16 [3584, 128], P('veh'), may hold values from -1.5 to 1.5
- crew_limit: float32 [128, 350], P('scen'), may hold values from -48 to 48
- crew_dual: float32 [128, 350], P('scen'), may hold values from 0 to 2
- crew_row: int32 [3584], P('veh'), may hold values from 0 to 349
- bundle_of: int32 [128, 1], replicated, may hold values from 0 to 7
- scen_weight: int32 [128], replicated, may hold values from 1 to 8
Outputs:
- new_plan: bfloat16 [128, 3584, 128], P('scen', 'veh')
- new_price: bfloat16 [128, 3584, 128], P('scen', 'veh')
- bundle_mean: bfloat16 [8, 3584, 128], P('scen', 'veh')
- new_dual: float32 [128, 350], P('scen')
- gap: float32 [], replicated
The draws below stay inside these ranges and needn't reach their ends.
Inputs may be any that keep to these rules, and one draw needn't show every extreme that they name: `bundle_of`: every bundle holds one scenario or more. `hessian`: symmetric.
All inputs are finite; a program needn't handle non-finite values.
Results may differ from the reference program's by a relative error of at most 0.0013.
The reference program's roundings to bfloat16 on the way (of `rounded`) count: a program that leaves them out, or rounds other values in their place, can miss the bound.
Values sent between devices are 32-bit elements; how exact they have to be, the bound alone decides.
A program may use at most 128 MiB of HBM per device.

```python
import jax
import jax.numpy as jnp
from jax import lax

NV = 128
CREW = 350
ITERS = 12
S = 128
NB = 8
V = 3584


def draw_hessian(key, part):
    key_off, key_diag = jax.random.split(key)
    raw_values = jax.random.uniform(key_off, (S, NV, NV), jnp.float32, -1.0, 1.0)
    limit_value = 3.8 / (NV - 1)
    symmetric = 0.5 * limit_value * (raw_values + jnp.swapaxes(raw_values, 1, 2))
    identity = jnp.eye(NV, dtype=jnp.float32)
    diagonal = jax.random.uniform(key_diag, (S, 1, NV), jnp.float32, 1.0, 3.0) + 3.8
    return (symmetric * (1.0 - identity) + identity * diagonal).astype(jnp.bfloat16)


def plant(drawn, key, smallest, largest):
    longest = drawn.shape.index(max(drawn.shape))
    spots = []
    for shift in (0, 1):
        where = [jax.random.randint(jax.random.fold_in(key, axis), (), 0, length) for axis, length in enumerate(drawn.shape)]
        where[longest] = (where[longest] + shift) % drawn.shape[longest]
        spots.append(tuple(where))
    return drawn.at[spots[0]].set(smallest).at[spots[1]].set(largest)


def block_levels(own_key, dims, cuts, least, high):
    level, own = 1.0, jax.random.fold_in(own_key, 6)
    for position, parts in cuts:
        heights = jnp.exp(jax.random.uniform(jax.random.fold_in(own, position), (parts,), jnp.float32, least / len(cuts), high / len(cuts)))
        level = level * jnp.repeat(heights, dims[position] // parts).reshape([-1 if axis == position else 1 for axis in range(len(dims))])
    return level


def distinct(key, rows, count, top, lift):
    ranking = jax.random.permutation(jax.random.fold_in(key, 1), count)
    boost = ranking
    for power in range(3):
        boost = boost * boost // count
    boost = boost * lift // count
    lots = jax.random.randint(jax.random.fold_in(key, 2), (rows, count), 0, 4096) + boost
    holders = jax.random.permutation(jax.random.fold_in(key, 3), rows)[jnp.arange(count) % rows]
    lots = jnp.where(jnp.arange(rows)[:, None] == holders[None, :], 1 << 14, lots)
    score = lots * count + jnp.arange(count)
    return lax.top_k(score.astype(jnp.int32), top)[1].astype(jnp.int32)


def centred(stream_key, dims, scale, reach, pieces=(), kind=jnp.bfloat16):
    array = jax.random.normal(stream_key, dims, jnp.float32) * scale
    if len(pieces) > 0:
        array = block_levels(stream_key, dims, pieces, -0.22, 0.18) * array
    return jnp.clip(array, min=-reach, max=reach).astype(kind)


def setup_inputs(seed: int = 0) -> dict:
    keys = jax.random.split(jax.random.key(seed), 12)
    return {
        "start_plan": centred(keys[0], (S, V, NV), 1.0, 6.0, ((0, 8), (1, 4))),
        "linear_cost": centred(keys[1], (S, V, NV), 2.0, 12.0, ((0, 8), (1, 4))),
        "price": centred(keys[2], (S, V, NV), 1.0, 6.0, ((0, 8), (1, 4))),
        "anchor": centred(keys[3], (NB, V, NV), 1.0, 6.0, ((1, 4),)),
        "hessian": draw_hessian(jax.random.fold_in(keys[11], 71), 0),
        "usage_coef": centred(keys[5], (V, NV), 0.25, 1.5, ((0, 4),)),
        "crew_limit": centred(keys[6], (S, CREW), 8.0, 48.0, ((0, 8),), jnp.float32),
        "crew_dual": jnp.clip(2.0 * jax.random.uniform(keys[7], (S, CREW), jnp.float32) ** block_levels(keys[7], (S, CREW), ((0, 8),), -0.2, 0.2), 0.0, 2.0),
        "crew_row": plant(jax.random.randint(keys[8], (V,), 0, CREW), jax.random.fold_in(keys[8], 1), 0, CREW - 1).astype(jnp.int32),
        "bundle_of": distinct(keys[9], S, NB, 1, 2048),
        "scen_weight": plant(jax.random.randint(keys[10], (S,), 1, 9), jax.random.fold_in(keys[10], 1), 1, 8).astype(jnp.int32),
    }


penalty = 1.0
step_size = 0.02
dual_step = 0.02
highest = lax.Precision.HIGHEST

def reference(start_plan, linear_cost, price, anchor, hessian, usage_coef, crew_limit, crew_dual, crew_row, bundle_of, scen_weight):
    bundles = bundle_of[:, 0]
    weights = scen_weight.astype(jnp.float32)
    coefficient = usage_coef.astype(jnp.float32)
    crew_map = (crew_row[:, None] == jnp.arange(CREW, dtype=jnp.int32)[None, :]).astype(jnp.float32)

    def solve_one(inputs):
        start_one, cost_one, price_one, bundle_one, hess_one, limit_one, dual_one = inputs
        anchored = lax.dynamic_index_in_dim(anchor, bundle_one, 0, keepdims=False).astype(jnp.float32)
        linear_part = cost_one.astype(jnp.float32) + price_one.astype(jnp.float32) - penalty * anchored
        hess_wide = hess_one.astype(jnp.float32)

        def advance(index, state_pair):
            roster, multiplier = state_pair
            rounded = lax.optimization_barrier(roster.astype(jnp.bfloat16)).astype(jnp.float32)
            curvature = jnp.dot(rounded, hess_wide, precision=highest)
            consumed = lax.optimization_barrier(jnp.sum(roster * coefficient, axis=1))
            usage = jnp.dot(consumed, crew_map, precision=highest)
            updated = jnp.maximum(multiplier + dual_step * (usage - limit_one), 0.0)
            per_vehicle = jnp.dot(crew_map, multiplier, precision=highest)
            gradient = curvature + linear_part + penalty * roster + per_vehicle[:, None] * coefficient
            return (roster - step_size * gradient, updated)
        return lax.fori_loop(0, ITERS, advance, (start_one.astype(jnp.float32), dual_one))
    roster, multiplier = lax.map(solve_one, (start_plan, linear_cost, price, bundles, hessian, crew_limit, crew_dual))
    selector = (bundles[:, None] == jnp.arange(NB, dtype=jnp.int32)[None, :]).astype(jnp.float32)
    bundle_weight = lax.optimization_barrier(jnp.sum(selector * weights[:, None], axis=0))
    totals = jnp.einsum('sb,svi->bvi', selector * weights[:, None], roster, precision=highest)
    mean_all = totals / bundle_weight[:, None, None]
    mean_here = jnp.einsum('sb,bvi->svi', selector, mean_all, precision=highest)
    deviation = roster - mean_here
    new_price = (price.astype(jnp.float32) + penalty * deviation).astype(jnp.bfloat16)
    spread = jnp.sum(weights * lax.optimization_barrier(jnp.sum(deviation * deviation, axis=(1, 2))))
    gap = jnp.sqrt(spread / (jnp.sum(weights) * V * NV))
    return (roster.astype(jnp.bfloat16), new_price, mean_all.astype(jnp.bfloat16), multiplier, gap)
```

```python
import functools

import jax
import jax.numpy as jnp
from jax import lax
from jax.experimental import pallas as pl
from jax.experimental.pallas import tpu as pltpu
from jax.sharding import PartitionSpec as P

ITERS = 12


penalty = 1.0
step_size = 0.02
dual_step = 0.02
highest = lax.Precision.HIGHEST
MESH = pl.DeviceIdType.MESH
LANES = 128


def halves(x):
    high = x.astype(jnp.bfloat16)
    return high, (x - high.astype(jnp.float32)).astype(jnp.bfloat16)


def steps_kernel(
    n,
    bundle_ref,
    start_ref,
    cost_ref,
    price_ref,
    anchor_ref,
    hess_ref,
    coef_ref,
    limit_ref,
    dual_ref,
    crew_ref,
    roster_ref,
    dual_out_ref,
    linear_ref,
    wide_ref,
    map_ref,
    coef_wide_ref,
    picked_ref,
    eaten_ref,
    use_ref,
    send_sem,
    recv_sem,
):
    me = lax.axis_index("veh")
    scen, rows, width = start_ref.shape
    crews = map_ref.shape[1]
    chunk = 64 if rows % 64 == 0 else rows

    barrier = pltpu.get_barrier_semaphore()
    for off in range(1, n):
        pl.semaphore_signal(
            barrier, inc=1, device_id={"veh": lax.rem(me + off, n)}, device_id_type=MESH
        )
    pl.semaphore_wait(barrier, n - 1)

    def outgoing(k, off):
        return pltpu.make_async_remote_copy(
            src_ref=use_ref.at[k, me],
            dst_ref=use_ref.at[k, me],
            send_sem=send_sem.at[k, off - 1],
            recv_sem=recv_sem.at[k, off - 1],
            device_id={"veh": lax.rem(me + off, n)},
            device_id_type=MESH,
        )

    def incoming(k, off):
        source = lax.rem(me + n - off, n)
        return pltpu.make_async_remote_copy(
            src_ref=use_ref.at[k, source],
            dst_ref=use_ref.at[k, source],
            send_sem=send_sem.at[k, off - 1],
            recv_sem=recv_sem.at[k, off - 1],
            device_id={"veh": lax.rem(me + off, n)},
            device_id_type=MESH,
        )

    map_ref[...] = jnp.where(
        crew_ref[...] == lax.broadcasted_iota(jnp.int32, (rows, crews), 1), 1.0, 0.0
    ).astype(jnp.bfloat16)
    coef_wide_ref[...] = coef_ref[...].astype(jnp.float32)
    eaten_ref[...] = jnp.zeros_like(eaten_ref)
    picked_ref[...] = jnp.zeros_like(picked_ref)
    dual_out_ref[...] = dual_ref[...]

    def lane_is(s):
        lanes = lax.broadcasted_iota(jnp.int32, (chunk, LANES), 1)
        return (lanes == s) | (lanes == s + scen)

    def prepare(s, carry):
        wide_ref[s, 0:width, 0:width] = hess_ref[s]
        wide_ref[s, 0:width, width:] = jnp.zeros((width, LANES), jnp.bfloat16)
        wide_ref[s, width:, 0:width] = jnp.zeros((LANES, width), jnp.bfloat16)
        row = lax.broadcasted_iota(jnp.int32, (LANES, LANES), 0)
        wide_ref[s, width:, width:] = jnp.where(
            (row == s) | (row == s + scen), 1.0, 0.0
        ).astype(jnp.bfloat16)
        mine = bundle_ref[s]
        mask = lane_is(s)
        for lo in range(0, rows, chunk):
            part = slice(lo, lo + chunk)
            linear_ref[s, part] = (
                cost_ref[s, part].astype(jnp.float32)
                + price_ref[s, part].astype(jnp.float32)
                - penalty * anchor_ref[mine, part].astype(jnp.float32)
            )
            roster = start_ref[s, part].astype(jnp.float32)
            roster_ref[s, part] = roster
            eaten = jnp.sum(roster * coef_wide_ref[part], axis=1, keepdims=True)
            eaten_ref[part] = jnp.where(mask, eaten, eaten_ref[part])
        return carry

    def share(k):
        high, low = halves(eaten_ref[...])
        lanes = lax.broadcasted_iota(jnp.int32, high.shape, 1)
        both = jnp.where(
            lanes < scen, high.astype(jnp.float32), low.astype(jnp.float32)
        ).astype(jnp.bfloat16)
        summed = lax.dot_general(
            both, map_ref[...], (((0,), (0,)), ((), ())), preferred_element_type=jnp.float32
        )
        use_ref[k, me] = summed[0:scen] + summed[scen : 2 * scen]
        for off in range(1, n):
            outgoing(k, off).start()

    def collect(k):
        for off in range(1, n):
            incoming(k, off).wait_recv()
        usage = use_ref[k, 0]
        for other in range(1, n):
            usage = usage + use_ref[k, other]
        dual_out_ref[...] = jnp.maximum(
            dual_out_ref[...] + dual_step * (usage - limit_ref[...]), 0.0
        )

    lax.fori_loop(0, scen, prepare, 0)
    share(0)

    def advance(k, carry):
        @pl.when(k > 0)
        def _():
            collect(k - 1)

        high, low = halves(dual_out_ref[...])
        pieces = jnp.concatenate([high, low], axis=0)
        picked_ref[:, 0 : 2 * scen] = lax.dot_general(
            map_ref[...], pieces, (((1,), (1,)), ((), ())), preferred_element_type=jnp.float32
        ).astype(jnp.bfloat16)

        def one(s, inner):
            left = jnp.concatenate([roster_ref[s].astype(jnp.bfloat16), picked_ref[...]], axis=1)
            both = jnp.dot(left, wide_ref[s], preferred_element_type=jnp.float32)
            mask = lane_is(s)
            for lo in range(0, rows, chunk):
                part = slice(lo, lo + chunk)
                coef = coef_wide_ref[part]
                roster = roster_ref[s, part]
                gradient = (
                    both[part, 0:width]
                    + linear_ref[s, part]
                    + penalty * roster
                    + both[part, width:] * coef
                )
                roster = roster - step_size * gradient
                roster_ref[s, part] = roster
                eaten = jnp.sum(roster * coef, axis=1, keepdims=True)
                eaten_ref[part] = jnp.where(mask, eaten, eaten_ref[part])
            return inner

        lax.fori_loop(0, scen, one, 0)

        @pl.when(k < ITERS - 1)
        def _():
            share(k + 1)

        return carry

    lax.fori_loop(0, ITERS, advance, 0)
    collect(ITERS - 1)

    def drain(k, carry):
        for off in range(1, n):
            outgoing(k, off).wait_send()
        return carry

    lax.fori_loop(0, ITERS, drain, 0)


def run_steps(start_plan, linear_cost, price, anchor, hessian, usage_coef, crew_limit, crew_dual, crew_row, my_bundles):
    n = lax.axis_size("veh")
    scen, rows, width = start_plan.shape
    crew_count = crew_limit.shape[1]
    crews = -(-crew_count // LANES) * LANES
    extra = ((0, 0), (0, crews - crew_count))
    vmem = pl.BlockSpec(memory_space=pltpu.VMEM)
    roster, dual = pl.pallas_call(
        functools.partial(steps_kernel, n),
        out_shape=(
            jax.ShapeDtypeStruct((scen, rows, width), jnp.float32),
            jax.ShapeDtypeStruct((scen, crews), jnp.float32),
        ),
        in_specs=[pl.BlockSpec(memory_space=pltpu.SMEM)] + [vmem] * 9,
        out_specs=(vmem, vmem),
        scratch_shapes=[
            pltpu.VMEM((scen, rows, width), jnp.float32),
            pltpu.VMEM((scen, width + LANES, width + LANES), jnp.bfloat16),
            pltpu.VMEM((rows, crews), jnp.bfloat16),
            pltpu.VMEM((rows, width), jnp.float32),
            pltpu.VMEM((rows, LANES), jnp.bfloat16),
            pltpu.VMEM((rows, LANES), jnp.float32),
            pltpu.VMEM((ITERS, n, scen, crews), jnp.float32),
            pltpu.SemaphoreType.DMA((ITERS, n - 1)),
            pltpu.SemaphoreType.DMA((ITERS, n - 1)),
        ],
        compiler_params=pltpu.CompilerParams(
            collective_id=0, has_side_effects=True, vmem_limit_bytes=62 * 1024 * 1024
        ),
    )(
        my_bundles,
        start_plan,
        linear_cost,
        price,
        anchor,
        hessian,
        usage_coef,
        jnp.pad(crew_limit, extra),
        jnp.pad(crew_dual, extra),
        crew_row[:, None],
    )
    return roster, dual[:, :crew_count]


def bit_of(index, bit):
    return lax.rem(lax.div(index, 2**bit), 2)


def spans(bits):
    out = [0]
    for bit in bits:
        out = out + [value + 2**bit for value in out]
    return out


def consensus_kernel(
    n_scen,
    n_veh,
    pieces,
    bundle_ref,
    pick_ref,
    weight_ref,
    every_ref,
    scale_ref,
    roster_ref,
    price_ref,
    plan_out,
    price_out,
    mean_out,
    gap_out,
    part_ref,
    land_ref,
    spread_ref,
    near_ref,
    far_ref,
    send_sem,
    recv_sem,
    side_send,
    side_recv,
    *mean_refs,
):
    me = lax.axis_index("scen")
    my_veh = lax.axis_index("veh")
    scen, rows, width = roster_ref.shape
    owned = mean_out.shape[0]
    bundles = part_ref.shape[0]
    bits = n_scen.bit_length() - 1
    size = rows // pieces
    half = size // 2 if size % 16 == 0 else size
    plain = list(range(bits))
    turned = plain[:1] + plain[:0:-1]

    barrier = pltpu.get_barrier_semaphore()
    for off in range(1, n_scen):
        pl.semaphore_signal(
            barrier, inc=1, device_id={"scen": lax.rem(me + off, n_scen)}, device_id_type=MESH
        )
    for off in range(1, n_veh):
        pl.semaphore_signal(
            barrier, inc=1, device_id={"veh": lax.rem(my_veh + off, n_veh)}, device_id_type=MESH
        )
    pl.semaphore_wait(barrier, n_scen + n_veh - 2)

    def partner(bit):
        return me + 2**bit - 2 ** (bit + 1) * bit_of(me, bit)

    def base_of(index, free):
        value = index
        for bit in free:
            value = value - 2**bit * bit_of(index, bit)
        return value

    def part_of(q):
        return pl.ds(q * size, size)

    def copies(q, stage):
        order = plain if q % 2 == 0 else turned
        down = stage < bits
        level = stage if down else 2 * bits - 1 - stage
        bit = order[level]
        free = order[level + 1 :]
        offsets = spans(free)
        found = []
        slot = sum(2 ** (bits - 1 - earlier) for earlier in range(level))
        for place, offset in enumerate(offsets):
            sem = (q * 2 + (0 if down else 1)) * (n_scen - 1) + slot + place
            other = partner(bit)
            if down:
                target = (base_of(other, free) + offset) * owned
                source = part_ref.at[pl.ds(target, owned), part_of(q)]
                goal = land_ref.at[slot + place, :, part_of(q)]
                mine = goal
            else:
                held = (base_of(me, free) + offset) * owned
                theirs = (base_of(other, free) + offset) * owned
                source = mean_refs[q].at[pl.ds(held, owned)]
                goal = source
                mine = mean_refs[q].at[pl.ds(theirs, owned)]
            out = functools.partial(
                pltpu.make_async_remote_copy,
                src_ref=source,
                dst_ref=goal,
                send_sem=send_sem.at[sem],
                recv_sem=recv_sem.at[sem],
                device_id={"scen": other},
                device_id_type=MESH,
            )
            back = functools.partial(
                pltpu.make_async_remote_copy,
                src_ref=source,
                dst_ref=mine,
                send_sem=send_sem.at[sem],
                recv_sem=recv_sem.at[sem],
                device_id={"scen": other},
                device_id_type=MESH,
            )
            keep = (base_of(me, free) + offset) * owned
            found.append((out, back, slot + place, keep))
        return found

    def launch(q, stage):
        for out, _, _, _ in copies(q, stage):
            out().start()

    def absorb(q, stage):
        for _, back, slot, keep in copies(q, stage):
            back().wait_recv()
            if stage < bits:
                for one in range(owned):
                    part_ref[keep + one, part_of(q)] += land_ref[slot, one, part_of(q)]

    def sums(q):
        def one(b, carry):
            for lo in range(0, size, half):
                where = pl.ds(q * size + lo, half)
                total = pick_ref[b, 0] * roster_ref[0, where]
                for s in range(1, scen):
                    total = total + pick_ref[b, s] * roster_ref[s, where]
                part_ref[b, where] = total
            return carry

        lax.fori_loop(0, bundles, one, 0)

    def settle(q):
        for one in range(owned):
            b = me * owned + one
            mean = part_ref[b, part_of(q)] / every_ref[b]
            mean_refs[q][b] = mean
            mean_out[one, part_of(q)] = mean.astype(jnp.bfloat16)

    def finish(q):
        def one(s, total):
            roster = roster_ref[s, part_of(q)]
            deviation = roster - mean_refs[q][bundle_ref[s]]
            plan_out[s, part_of(q)] = roster.astype(jnp.bfloat16)
            price_out[s, part_of(q)] = (
                price_ref[s, part_of(q)].astype(jnp.float32) + penalty * deviation
            ).astype(jnp.bfloat16)
            square = jnp.sum((deviation * deviation).reshape(size // 8, 8, width), axis=0)
            return total + weight_ref[s] * square

        spread_ref[...] = lax.fori_loop(0, scen, one, spread_ref[...])

    spread_ref[...] = jnp.zeros_like(spread_ref)
    for turn in range(pieces + 2 * bits):
        for stage in range(2 * bits + 1):
            q = turn - stage
            if q < 0 or q >= pieces:
                continue
            if stage == 0:
                sums(q)
            else:
                absorb(q, stage - 1)
            if stage == bits:
                settle(q)
            if stage < 2 * bits:
                launch(q, stage)
            else:
                finish(q)

    near_ref[me] = spread_ref[...]
    steps = []
    for axis, here, count, ref, first in (
        ("scen", me, n_scen, near_ref, 0),
        ("veh", my_veh, n_veh, far_ref, n_scen - 1),
    ):
        sent = []
        if axis == "veh":
            total = near_ref[0]
            for other in range(1, n_scen):
                total = total + near_ref[other]
            far_ref[my_veh] = total
        for off in range(1, count):
            sem = first + off - 1
            out = pltpu.make_async_remote_copy(
                src_ref=ref.at[here],
                dst_ref=ref.at[here],
                send_sem=side_send.at[sem],
                recv_sem=side_recv.at[sem],
                device_id={axis: lax.rem(here + off, count)},
                device_id_type=MESH,
            )
            out.start()
            sent.append(out)
        for off in range(1, count):
            sem = first + off - 1
            origin = lax.rem(here + count - off, count)
            pltpu.make_async_remote_copy(
                src_ref=ref.at[origin],
                dst_ref=ref.at[origin],
                send_sem=side_send.at[sem],
                recv_sem=side_recv.at[sem],
                device_id={axis: lax.rem(here + off, count)},
                device_id_type=MESH,
            ).wait_recv()
        steps = steps + sent
    total = far_ref[0]
    for other in range(1, n_veh):
        total = total + far_ref[other]
    whole = jnp.sum(jnp.sum(total, axis=1, keepdims=True), axis=0, keepdims=True)
    gap_out[...] = jnp.sqrt(jnp.broadcast_to(whole, gap_out.shape) / scale_ref[0])

    for out in steps:
        out.wait_send()
    for q in range(pieces):
        for stage in range(2 * bits):
            for out, _, _, _ in copies(q, stage):
                out().wait_send()


def run_consensus(roster, price, my_bundles, pick, my_weights, every_weight, scale, bundles):
    n_scen, n_veh = lax.axis_size("scen"), lax.axis_size("veh")
    scen, rows, width = roster.shape
    owned = bundles // n_scen
    pieces = 8
    while rows % (8 * pieces):
        pieces = pieces // 2
    vmem = pl.BlockSpec(memory_space=pltpu.VMEM)
    smem = pl.BlockSpec(memory_space=pltpu.SMEM)
    copies = pieces * 2 * (n_scen - 1)
    side = n_scen + n_veh - 2
    f32, bf16 = jnp.float32, jnp.bfloat16
    return pl.pallas_call(
        functools.partial(consensus_kernel, n_scen, n_veh, pieces),
        out_shape=(
            jax.ShapeDtypeStruct((scen, rows, width), bf16),
            jax.ShapeDtypeStruct((scen, rows, width), bf16),
            jax.ShapeDtypeStruct((owned, rows, width), bf16),
            jax.ShapeDtypeStruct((8, LANES), f32),
        ),
        in_specs=[smem] * 5 + [vmem] * 2,
        out_specs=(vmem,) * 4,
        scratch_shapes=[
            pltpu.VMEM((bundles, rows, width), f32),
            pltpu.VMEM((n_scen - 1, owned, rows, width), f32),
            pltpu.VMEM((8, width), f32),
            pltpu.VMEM((n_scen, 8, width), f32),
            pltpu.VMEM((n_veh, 8, width), f32),
            pltpu.SemaphoreType.DMA((copies,)),
            pltpu.SemaphoreType.DMA((copies,)),
            pltpu.SemaphoreType.DMA((side,)),
            pltpu.SemaphoreType.DMA((side,)),
        ]
        + [pltpu.VMEM((bundles, rows // pieces, width), f32)] * pieces,
        compiler_params=pltpu.CompilerParams(
            collective_id=1, has_side_effects=True, vmem_limit_bytes=62 * 1024 * 1024
        ),
    )(my_bundles, pick, my_weights, every_weight, scale, roster, price)


def shards(
    start_plan,
    linear_cost,
    price,
    anchor,
    hessian,
    usage_coef,
    crew_limit,
    crew_dual,
    crew_row,
    bundle_of,
    scen_weight,
):
    local_scen = start_plan.shape[0]
    bundle_count = anchor.shape[0]
    offset = lax.axis_index("scen") * local_scen
    all_bundles = bundle_of[:, 0]
    my_bundles = lax.dynamic_slice_in_dim(all_bundles, offset, local_scen)
    my_weights = lax.dynamic_slice_in_dim(scen_weight, offset, local_scen).astype(jnp.float32)
    bundle_ids = jnp.arange(bundle_count, dtype=jnp.int32)
    selector = (my_bundles[:, None] == bundle_ids[None, :]).astype(jnp.float32)

    roster, multiplier = run_steps(
        start_plan, linear_cost, price, anchor, hessian, usage_coef,
        crew_limit, crew_dual, crew_row, my_bundles,
    )
    weighted_pick = selector * my_weights[:, None]
    every_weight = jnp.sum(
        (all_bundles[:, None] == bundle_ids[None, :]).astype(jnp.float32)
        * scen_weight.astype(jnp.float32)[:, None],
        axis=0,
    )
    entries = start_plan.shape[1] * lax.axis_size("veh") * start_plan.shape[2]
    scale = (jnp.sum(scen_weight.astype(jnp.float32)) * entries)[None]
    plan, new_price, own_mean, gap = run_consensus(
        roster, price, my_bundles, weighted_pick.T, my_weights, every_weight, scale, bundle_count
    )
    return (plan, new_price, own_mean, multiplier, gap[0, 0])


def solution(mesh):
    return jax.shard_map(
        shards,
        mesh=mesh,
        in_specs=(
            P("scen", "veh", None),
            P("scen", "veh", None),
            P("scen", "veh", None),
            P(None, "veh", None),
            P("scen", None, None),
            P("veh", None),
            P("scen", None),
            P("scen", None),
            P("veh"),
            P(),
            P(),
        ),
        out_specs=(
            P("scen", "veh", None),
            P("scen", "veh", None),
            P("scen", "veh", None),
            P("scen", None),
            P(),
        ),
        check_vma=False,
    )
```

```python
import functools
import math

import jax
import jax.numpy as jnp
from jax import lax
from jax.experimental import pallas as pl
from jax.experimental.pallas import tpu as pltpu
from jax.sharding import PartitionSpec as P

ITERS = 12


penalty = 1.0
step_size = 0.02
dual_step = 0.02
highest = lax.Precision.HIGHEST
MESH = pl.DeviceIdType.MESH
LANES = 128
GROUP = 4


def halves(x):
    high = x.astype(jnp.bfloat16)
    return high, (x - high.astype(jnp.float32)).astype(jnp.bfloat16)


def steps_kernel(
    n,
    bundle_ref,
    start_ref,
    cost_ref,
    price_ref,
    anchor_ref,
    hess_ref,
    coef_ref,
    limit_ref,
    dual_ref,
    crew_ref,
    roster_ref,
    dual_out_ref,
    linear_ref,
    wide_ref,
    map_ref,
    coef_wide_ref,
    picked_ref,
    eaten_ref,
    use_ref,
    send_sem,
    recv_sem,
):
    me = lax.axis_index("veh")
    scen, rows, width = start_ref.shape
    crews = map_ref.shape[1]
    together = math.gcd(scen, GROUP)
    chunk = 32 if rows % 32 == 0 else rows

    barrier = pltpu.get_barrier_semaphore()
    for off in range(1, n):
        pl.semaphore_signal(
            barrier, inc=1, device_id={"veh": lax.rem(me + off, n)}, device_id_type=MESH
        )
    pl.semaphore_wait(barrier, n - 1)

    def outgoing(k, off):
        return pltpu.make_async_remote_copy(
            src_ref=use_ref.at[k, me],
            dst_ref=use_ref.at[k, me],
            send_sem=send_sem.at[k, off - 1],
            recv_sem=recv_sem.at[k, off - 1],
            device_id={"veh": lax.rem(me + off, n)},
            device_id_type=MESH,
        )

    def incoming(k, off):
        source = lax.rem(me + n - off, n)
        return pltpu.make_async_remote_copy(
            src_ref=use_ref.at[k, source],
            dst_ref=use_ref.at[k, source],
            send_sem=send_sem.at[k, off - 1],
            recv_sem=recv_sem.at[k, off - 1],
            device_id={"veh": lax.rem(me + off, n)},
            device_id_type=MESH,
        )

    map_ref[...] = jnp.where(
        crew_ref[...] == lax.broadcasted_iota(jnp.int32, (rows, crews), 1), 1.0, 0.0
    ).astype(jnp.bfloat16)
    coef_wide_ref[...] = coef_ref[...].astype(jnp.float32)
    eaten_ref[...] = jnp.zeros_like(eaten_ref)
    picked_ref[...] = jnp.zeros_like(picked_ref)
    dual_out_ref[...] = dual_ref[...]

    def lane_is(s):
        lanes = lax.broadcasted_iota(jnp.int32, (chunk, LANES), 1)
        return (lanes == s) | (lanes == s + scen)

    def prepare(s, carry):
        wide_ref[s, 0:width, 0:width] = hess_ref[s]
        wide_ref[s, 0:width, width:] = jnp.zeros((width, LANES), jnp.bfloat16)
        wide_ref[s, width:, 0:width] = jnp.zeros((LANES, width), jnp.bfloat16)
        row = lax.broadcasted_iota(jnp.int32, (LANES, LANES), 0)
        wide_ref[s, width:, width:] = jnp.where(
            (row == s) | (row == s + scen), 1.0, 0.0
        ).astype(jnp.bfloat16)
        mine = bundle_ref[s]
        mask = lane_is(s)
        for lo in range(0, rows, chunk):
            part = slice(lo, lo + chunk)
            linear_ref[s, part] = (
                cost_ref[s, part].astype(jnp.float32)
                + price_ref[s, part].astype(jnp.float32)
                - penalty * anchor_ref[mine, part].astype(jnp.float32)
            )
            roster = start_ref[s, part].astype(jnp.float32)
            roster_ref[s, part] = roster
            eaten = jnp.sum(roster * coef_wide_ref[part], axis=1, keepdims=True)
            eaten_ref[part] = jnp.where(mask, eaten, eaten_ref[part])
        return carry

    def share(k):
        high, low = halves(eaten_ref[...])
        lanes = lax.broadcasted_iota(jnp.int32, high.shape, 1)
        both = jnp.where(
            lanes < scen, high.astype(jnp.float32), low.astype(jnp.float32)
        ).astype(jnp.bfloat16)
        summed = lax.dot_general(
            both, map_ref[...], (((0,), (0,)), ((), ())), preferred_element_type=jnp.float32
        )
        use_ref[k, me] = summed[0:scen] + summed[scen : 2 * scen]
        for off in range(1, n):
            outgoing(k, off).start()

    def collect(k):
        for off in range(1, n):
            incoming(k, off).wait_recv()
        usage = use_ref[k, 0]
        for other in range(1, n):
            usage = usage + use_ref[k, other]
        dual_out_ref[...] = jnp.maximum(
            dual_out_ref[...] + dual_step * (usage - limit_ref[...]), 0.0
        )

    lax.fori_loop(0, scen, prepare, 0)
    share(0)

    def advance(k, carry):
        @pl.when(k > 0)
        def _():
            collect(k - 1)

        high, low = halves(dual_out_ref[...])
        pieces = jnp.concatenate([high, low], axis=0)
        picked_ref[:, 0 : 2 * scen] = lax.dot_general(
            map_ref[...], pieces, (((1,), (1,)), ((), ())), preferred_element_type=jnp.float32
        ).astype(jnp.bfloat16)

        def several(group, inner):
            chosen = [group * together + extra for extra in range(together)]
            results = [
                jnp.dot(
                    jnp.concatenate(
                        [roster_ref[s].astype(jnp.bfloat16), picked_ref[...]], axis=1
                    ),
                    wide_ref[s],
                    preferred_element_type=jnp.float32,
                )
                for s in chosen
            ]
            masks = [lane_is(s) for s in chosen]
            for lo in range(0, rows, chunk):
                part = slice(lo, lo + chunk)
                coef = coef_wide_ref[part]
                gathered = eaten_ref[part]
                for s, both, mask in zip(chosen, results, masks):
                    roster = roster_ref[s, part]
                    gradient = (
                        both[part, 0:width]
                        + linear_ref[s, part]
                        + penalty * roster
                        + both[part, width:] * coef
                    )
                    roster = roster - step_size * gradient
                    roster_ref[s, part] = roster
                    eaten = jnp.sum(roster * coef, axis=1, keepdims=True)
                    gathered = jnp.where(mask, eaten, gathered)
                eaten_ref[part] = gathered
            return inner

        lax.fori_loop(0, scen // together, several, 0)

        @pl.when(k < ITERS - 1)
        def _():
            share(k + 1)

        return carry

    lax.fori_loop(0, ITERS, advance, 0)
    collect(ITERS - 1)

    def drain(k, carry):
        for off in range(1, n):
            outgoing(k, off).wait_send()
        return carry

    lax.fori_loop(0, ITERS, drain, 0)


def run_steps(start_plan, linear_cost, price, anchor, hessian, usage_coef, crew_limit, crew_dual, crew_row, my_bundles):
    n = lax.axis_size("veh")
    scen, rows, width = start_plan.shape
    crew_count = crew_limit.shape[1]
    crews = -(-crew_count // LANES) * LANES
    extra = ((0, 0), (0, crews - crew_count))
    vmem = pl.BlockSpec(memory_space=pltpu.VMEM)
    roster, dual = pl.pallas_call(
        functools.partial(steps_kernel, n),
        out_shape=(
            jax.ShapeDtypeStruct((scen, rows, width), jnp.float32),
            jax.ShapeDtypeStruct((scen, crews), jnp.float32),
        ),
        in_specs=[pl.BlockSpec(memory_space=pltpu.SMEM)] + [vmem] * 9,
        out_specs=(vmem, vmem),
        scratch_shapes=[
            pltpu.VMEM((scen, rows, width), jnp.float32),
            pltpu.VMEM((scen, width + LANES, width + LANES), jnp.bfloat16),
            pltpu.VMEM((rows, crews), jnp.bfloat16),
            pltpu.VMEM((rows, width), jnp.float32),
            pltpu.VMEM((rows, LANES), jnp.bfloat16),
            pltpu.VMEM((rows, LANES), jnp.float32),
            pltpu.VMEM((ITERS, n, scen, crews), jnp.float32),
            pltpu.SemaphoreType.DMA((ITERS, n - 1)),
            pltpu.SemaphoreType.DMA((ITERS, n - 1)),
        ],
        compiler_params=pltpu.CompilerParams(
            collective_id=0, has_side_effects=True, vmem_limit_bytes=62 * 1024 * 1024
        ),
    )(
        my_bundles,
        start_plan,
        linear_cost,
        price,
        anchor,
        hessian,
        usage_coef,
        jnp.pad(crew_limit, extra),
        jnp.pad(crew_dual, extra),
        crew_row[:, None],
    )
    return roster, dual[:, :crew_count]


def bit_of(index, bit):
    return lax.rem(lax.div(index, 2**bit), 2)


def spans(bits):
    out = [0]
    for bit in bits:
        out = out + [value + 2**bit for value in out]
    return out


def consensus_kernel(
    n_scen,
    n_veh,
    pieces,
    bundle_ref,
    pick_ref,
    weight_ref,
    every_ref,
    scale_ref,
    roster_ref,
    price_ref,
    plan_out,
    price_out,
    mean_out,
    gap_out,
    part_ref,
    land_ref,
    spread_ref,
    near_ref,
    far_ref,
    send_sem,
    recv_sem,
    side_send,
    side_recv,
    *mean_refs,
):
    me = lax.axis_index("scen")
    my_veh = lax.axis_index("veh")
    scen, rows, width = roster_ref.shape
    owned = mean_out.shape[0]
    bundles = part_ref.shape[0]
    bits = n_scen.bit_length() - 1
    size = rows // pieces
    half = size // 2 if size % 16 == 0 else size
    plain = list(range(bits))
    turned = plain[:1] + plain[:0:-1]

    barrier = pltpu.get_barrier_semaphore()
    for off in range(1, n_scen):
        pl.semaphore_signal(
            barrier, inc=1, device_id={"scen": lax.rem(me + off, n_scen)}, device_id_type=MESH
        )
    for off in range(1, n_veh):
        pl.semaphore_signal(
            barrier, inc=1, device_id={"veh": lax.rem(my_veh + off, n_veh)}, device_id_type=MESH
        )
    pl.semaphore_wait(barrier, n_scen + n_veh - 2)

    def partner(bit):
        return me + 2**bit - 2 ** (bit + 1) * bit_of(me, bit)

    def base_of(index, free):
        value = index
        for bit in free:
            value = value - 2**bit * bit_of(index, bit)
        return value

    def part_of(q):
        return pl.ds(q * size, size)

    def copies(q, stage):
        order = plain if q % 2 == 0 else turned
        down = stage < bits
        level = stage if down else 2 * bits - 1 - stage
        bit = order[level]
        free = order[level + 1 :]
        offsets = spans(free)
        found = []
        slot = sum(2 ** (bits - 1 - earlier) for earlier in range(level))
        for place, offset in enumerate(offsets):
            sem = (q * 2 + (0 if down else 1)) * (n_scen - 1) + slot + place
            other = partner(bit)
            if down:
                target = (base_of(other, free) + offset) * owned
                source = part_ref.at[pl.ds(target, owned), part_of(q)]
                goal = land_ref.at[slot + place, :, part_of(q)]
                mine = goal
            else:
                held = (base_of(me, free) + offset) * owned
                theirs = (base_of(other, free) + offset) * owned
                source = mean_refs[q].at[pl.ds(held, owned)]
                goal = source
                mine = mean_refs[q].at[pl.ds(theirs, owned)]
            out = functools.partial(
                pltpu.make_async_remote_copy,
                src_ref=source,
                dst_ref=goal,
                send_sem=send_sem.at[sem],
                recv_sem=recv_sem.at[sem],
                device_id={"scen": other},
                device_id_type=MESH,
            )
            back = functools.partial(
                pltpu.make_async_remote_copy,
                src_ref=source,
                dst_ref=mine,
                send_sem=send_sem.at[sem],
                recv_sem=recv_sem.at[sem],
                device_id={"scen": other},
                device_id_type=MESH,
            )
            keep = (base_of(me, free) + offset) * owned
            found.append((out, back, slot + place, keep))
        return found

    def launch(q, stage):
        for out, _, _, _ in copies(q, stage):
            out().start()

    def absorb(q, stage):
        for _, back, slot, keep in copies(q, stage):
            back().wait_recv()
            if stage < bits:
                for one in range(owned):
                    part_ref[keep + one, part_of(q)] += land_ref[slot, one, part_of(q)]

    def sums(q):
        def one(b, carry):
            for lo in range(0, size, half):
                where = pl.ds(q * size + lo, half)
                total = pick_ref[b, 0] * roster_ref[0, where]
                for s in range(1, scen):
                    total = total + pick_ref[b, s] * roster_ref[s, where]
                part_ref[b, where] = total
            return carry

        lax.fori_loop(0, bundles, one, 0)

    def settle(q):
        for one in range(owned):
            b = me * owned + one
            mean = part_ref[b, part_of(q)] / every_ref[b]
            mean_refs[q][b] = mean
            mean_out[one, part_of(q)] = mean.astype(jnp.bfloat16)

    def finish(q):
        def one(s, total):
            roster = roster_ref[s, part_of(q)]
            deviation = roster - mean_refs[q][bundle_ref[s]]
            plan_out[s, part_of(q)] = roster.astype(jnp.bfloat16)
            price_out[s, part_of(q)] = (
                price_ref[s, part_of(q)].astype(jnp.float32) + penalty * deviation
            ).astype(jnp.bfloat16)
            square = jnp.sum((deviation * deviation).reshape(size // 8, 8, width), axis=0)
            return total + weight_ref[s] * square

        spread_ref[...] = lax.fori_loop(0, scen, one, spread_ref[...])

    spread_ref[...] = jnp.zeros_like(spread_ref)
    for turn in range(pieces + 2 * bits):
        for stage in range(2 * bits + 1):
            q = turn - stage
            if q < 0 or q >= pieces:
                continue
            if stage == 0:
                sums(q)
            else:
                absorb(q, stage - 1)
            if stage == bits:
                settle(q)
            if stage < 2 * bits:
                launch(q, stage)
            else:
                finish(q)

    near_ref[me] = spread_ref[...]
    steps = []
    for axis, here, count, ref, first in (
        ("scen", me, n_scen, near_ref, 0),
        ("veh", my_veh, n_veh, far_ref, n_scen - 1),
    ):
        sent = []
        if axis == "veh":
            total = near_ref[0]
            for other in range(1, n_scen):
                total = total + near_ref[other]
            far_ref[my_veh] = total
        for off in range(1, count):
            sem = first + off - 1
            out = pltpu.make_async_remote_copy(
                src_ref=ref.at[here],
                dst_ref=ref.at[here],
                send_sem=side_send.at[sem],
                recv_sem=side_recv.at[sem],
                device_id={axis: lax.rem(here + off, count)},
                device_id_type=MESH,
            )
            out.start()
            sent.append(out)
        for off in range(1, count):
            sem = first + off - 1
            origin = lax.rem(here + count - off, count)
            pltpu.make_async_remote_copy(
                src_ref=ref.at[origin],
                dst_ref=ref.at[origin],
                send_sem=side_send.at[sem],
                recv_sem=side_recv.at[sem],
                device_id={axis: lax.rem(here + off, count)},
                device_id_type=MESH,
            ).wait_recv()
        steps = steps + sent
    total = far_ref[0]
    for other in range(1, n_veh):
        total = total + far_ref[other]
    whole = jnp.sum(jnp.sum(total, axis=1, keepdims=True), axis=0, keepdims=True)
    gap_out[...] = jnp.sqrt(jnp.broadcast_to(whole, gap_out.shape) / scale_ref[0])

    for out in steps:
        out.wait_send()
    for q in range(pieces):
        for stage in range(2 * bits):
            for out, _, _, _ in copies(q, stage):
                out().wait_send()


def run_consensus(roster, price, my_bundles, pick, my_weights, every_weight, scale, bundles):
    n_scen, n_veh = lax.axis_size("scen"), lax.axis_size("veh")
    scen, rows, width = roster.shape
    owned = bundles // n_scen
    pieces = 8
    while rows % (8 * pieces):
        pieces = pieces // 2
    vmem = pl.BlockSpec(memory_space=pltpu.VMEM)
    smem = pl.BlockSpec(memory_space=pltpu.SMEM)
    copies = pieces * 2 * (n_scen - 1)
    side = n_scen + n_veh - 2
    f32, bf16 = jnp.float32, jnp.bfloat16
    return pl.pallas_call(
        functools.partial(consensus_kernel, n_scen, n_veh, pieces),
        out_shape=(
            jax.ShapeDtypeStruct((scen, rows, width), bf16),
            jax.ShapeDtypeStruct((scen, rows, width), bf16),
            jax.ShapeDtypeStruct((owned, rows, width), bf16),
            jax.ShapeDtypeStruct((8, LANES), f32),
        ),
        in_specs=[smem] * 5 + [vmem] * 2,
        out_specs=(vmem,) * 4,
        scratch_shapes=[
            pltpu.VMEM((bundles, rows, width), f32),
            pltpu.VMEM((n_scen - 1, owned, rows, width), f32),
            pltpu.VMEM((8, width), f32),
            pltpu.VMEM((n_scen, 8, width), f32),
            pltpu.VMEM((n_veh, 8, width), f32),
            pltpu.SemaphoreType.DMA((copies,)),
            pltpu.SemaphoreType.DMA((copies,)),
            pltpu.SemaphoreType.DMA((side,)),
            pltpu.SemaphoreType.DMA((side,)),
        ]
        + [pltpu.VMEM((bundles, rows // pieces, width), f32)] * pieces,
        compiler_params=pltpu.CompilerParams(
            collective_id=1, has_side_effects=True, vmem_limit_bytes=62 * 1024 * 1024
        ),
    )(my_bundles, pick, my_weights, every_weight, scale, roster, price)


def shards(
    start_plan,
    linear_cost,
    price,
    anchor,
    hessian,
    usage_coef,
    crew_limit,
    crew_dual,
    crew_row,
    bundle_of,
    scen_weight,
):
    local_scen = start_plan.shape[0]
    bundle_count = anchor.shape[0]
    offset = lax.axis_index("scen") * local_scen
    all_bundles = bundle_of[:, 0]
    my_bundles = lax.dynamic_slice_in_dim(all_bundles, offset, local_scen)
    my_weights = lax.dynamic_slice_in_dim(scen_weight, offset, local_scen).astype(jnp.float32)
    bundle_ids = jnp.arange(bundle_count, dtype=jnp.int32)
    selector = (my_bundles[:, None] == bundle_ids[None, :]).astype(jnp.float32)

    roster, multiplier = run_steps(
        start_plan, linear_cost, price, anchor, hessian, usage_coef,
        crew_limit, crew_dual, crew_row, my_bundles,
    )
    weighted_pick = selector * my_weights[:, None]
    every_weight = jnp.sum(
        (all_bundles[:, None] == bundle_ids[None, :]).astype(jnp.float32)
        * scen_weight.astype(jnp.float32)[:, None],
        axis=0,
    )
    entries = start_plan.shape[1] * lax.axis_size("veh") * start_plan.shape[2]
    scale = (jnp.sum(scen_weight.astype(jnp.float32)) * entries)[None]
    plan, new_price, own_mean, gap = run_consensus(
        roster, price, my_bundles, weighted_pick.T, my_weights, every_weight, scale, bundle_count
    )
    return (plan, new_price, own_mean, multiplier, gap[0, 0])


def solution(mesh):
    return jax.shard_map(
        shards,
        mesh=mesh,
        in_specs=(
            P("scen", "veh", None),
            P("scen", "veh", None),
            P("scen", "veh", None),
            P(None, "veh", None),
            P("scen", None, None),
            P("veh", None),
            P("scen", None),
            P("scen", None),
            P("veh"),
            P(),
            P(),
        ),
        out_specs=(
            P("scen", "veh", None),
            P("scen", "veh", None),
            P("scen", "veh", None),
            P("scen", None),
            P(),
        ),
        check_vma=False,
    )
```
